32 devices in a mesh: gx: 8 (over z, core), gy: 4 (over y, x).
Axes of the slice: x: 2, y: 2, z: 4, core: 2. Of those that a mesh axis runs over, the one named last changes fastest.
Arguments:
- base_state: float32 [3, 32, 32, 128], P(None, 'gx', 'gy'), may hold values from -5 to 5
- adjoint_block: float32 [32, 3, 32, 32, 128], P(None, None, 'gx', 'gy'), may hold values from -2500 to 2500
Outputs:
- q_block: float32 [32, 3, 32, 32, 128], P(None, None, 'gx', 'gy')
- r_factor: float32 [32, 32], replicated
The draws below stay inside these ranges and needn't reach their ends.
All inputs are finite; a program needn't handle non-finite values.
Results may differ from the reference program's by a relative error of at most 0.00015.
Values sent between devices are 32-bit elements; how exact they have to be, the bound alone decides.
A program may use at most 64 MiB of HBM per device.

```python
import math
import jax
import jax.numpy as jnp
from jax import lax

VECS = 32
NZ = 128
NX = 32
NY = 32


def draw_adjoint_block(key, part):
    keys = jax.random.split(jax.random.fold_in(key, 17), 7)
    shape = (VECS, 3, NX, NY, NZ)
    field_shape = (1, 3, NX, NY, NZ)
    noise = jnp.clip(jax.random.normal(keys[0], shape, jnp.float32), -5.0, 5.0)
    spread = 1.0
    common_one = jnp.clip(jax.random.normal(keys[1], field_shape, jnp.float32), -4.0, 4.0)
    common_two = jnp.clip(jax.random.normal(keys[2], field_shape, jnp.float32), -4.0, 4.0)
    mix_one = jax.random.uniform(keys[3], (VECS, 1, 1, 1, 1), jnp.float32, -spread, spread)
    mix_two = jax.random.uniform(keys[4], (VECS, 1, 1, 1, 1), jnp.float32, -spread, spread)
    row_scale = jnp.exp(jax.random.uniform(keys[5], (VECS, 1, 1, 1, 1), jnp.float32, 0.0, math.log(10.0)))
    along_x = jnp.arange(NX, dtype=jnp.float32)[:, None] / float(NX)
    along_y = jnp.arange(NY, dtype=jnp.float32)[None, :] / float(NY)
    exponent = 0.5 * along_x + 0.5 * along_y
    rough = jax.random.uniform(keys[6], (1, 1, NX, NY, 1), jnp.float32, 0.7, 1.4)
    spatial = jnp.exp(math.log(10.0) * exponent)[None, None, :, :, None] * rough
    return row_scale * spatial * (noise + mix_one * common_one + mix_two * common_two)


def steps_of(stream_key, dims, cuts, low, top_value):
    factor_of, own = 1.0, jax.random.fold_in(stream_key, 6)
    for dim, blocks in cuts:
        draws = jnp.exp(jax.random.uniform(jax.random.fold_in(own, dim), (blocks,), jnp.float32, low / len(cuts), top_value / len(cuts)))
        factor_of = factor_of * jnp.repeat(draws, dims[dim] // blocks).reshape([-1 if axis == dim else 1 for axis in range(len(dims))])
    return factor_of


def normal_values(rng, shape, scale, reach, pieces=(), kind=jnp.bfloat16):
    drawn = scale * jax.random.normal(rng, shape, jnp.float32)
    if pieces:
        drawn = drawn * steps_of(rng, shape, pieces, -0.22, 0.18)
    return jnp.clip(drawn, -reach, reach).astype(kind)


def setup_inputs(seed: int = 0) -> dict:
    arg_keys = jax.random.split(jax.random.key(seed), 3)
    return {
        "base_state": normal_values(arg_keys[0], (3, NX, NY, NZ), 1.0, 5.0, ((1, 8), (2, 4)), jnp.float32),
        "adjoint_block": draw_adjoint_block(jax.random.fold_in(arg_keys[2], 71), 0),
    }


ADVECT = 0.1
DIFFUSE = 0.08
DRIVE_SCALE = 0.25
WAVENUMBER = 4.0

def advance(padded, column_index, ny_total):
    centre = padded[:, 1:-1, 1:-1, :]
    eastern = padded[:, 2:, 1:-1, :]
    western = padded[:, :-2, 1:-1, :]
    northern = padded[:, 1:-1, 2:, :]
    southern = padded[:, 1:-1, :-2, :]
    upward = jnp.roll(centre, -1, axis=3)
    downward = jnp.roll(centre, 1, axis=3)
    laplacian = eastern + western + northern + southern + upward + downward - 6.0 * centre
    advection = centre[0:1] * (eastern - western) + centre[1:2] * (northern - southern) + centre[2:3] * (upward - downward)
    phases = 2.0 * math.pi * WAVENUMBER * column_index.astype(jnp.float32) / float(ny_total)
    forcing = DRIVE_SCALE * jnp.sin(phases)
    nothing = jnp.zeros_like(forcing)
    driven = jnp.stack([forcing, nothing, nothing])[:, None, :, None]
    return centre + DIFFUSE * laplacian - ADVECT * advection + driven

def adjoint(base_ext, block_ext):
    inner = block_ext[:, :, 1:-1, 1:-1, :]
    base_inner = base_ext[:, 1:-1, 1:-1, :]
    base_east = base_ext[:, 2:, 1:-1, :]
    base_west = base_ext[:, :-2, 1:-1, :]
    base_north = base_ext[:, 1:-1, 2:, :]
    base_south = base_ext[:, 1:-1, :-2, :]
    block_east = block_ext[:, :, 2:, 1:-1, :]
    block_west = block_ext[:, :, :-2, 1:-1, :]
    block_north = block_ext[:, :, 1:-1, 2:, :]
    block_south = block_ext[:, :, 1:-1, :-2, :]
    carried = base_inner[2] * inner
    flux = base_east[0] * block_east - base_west[0] * block_west
    flux = flux + base_north[1] * block_north - base_south[1] * block_south
    flux = flux + jnp.roll(carried, -1, axis=-1) - jnp.roll(carried, 1, axis=-1)
    grad_x = base_east - base_west
    grad_y = base_north - base_south
    grad_z = jnp.roll(base_inner, -1, axis=3) - jnp.roll(base_inner, 1, axis=3)
    coupling = jnp.stack([jnp.sum(inner * grad_x, axis=1), jnp.sum(inner * grad_y, axis=1), jnp.sum(inner * grad_z, axis=1)], axis=1)
    laplacian = block_east + block_west + block_north + block_south + jnp.roll(inner, -1, axis=-1) + jnp.roll(inner, 1, axis=-1) - 6.0 * inner
    return inner + ADVECT * (flux - coupling) + DIFFUSE * laplacian

def reference(base_state, adjoint_block):
    ny_total = base_state.shape[2]
    widths = ((0, 0), (1, 1), (1, 1), (0, 0))
    padded = jnp.pad(base_state, widths, mode='wrap')
    advanced = advance(padded, jnp.arange(ny_total, dtype=jnp.int32), ny_total)
    base_ext = jnp.pad(advanced, widths, mode='wrap')

    def one_vector(vector):
        extended = jnp.pad(vector, widths, mode='wrap')[None]
        return adjoint(base_ext, extended)[0]
    updated = lax.map(one_vector, adjoint_block)
    vectors = updated.shape[0]
    flat = updated.reshape(vectors, -1)
    gram = jnp.dot(flat.astype(jnp.float32), flat.T.astype(jnp.float32), precision=lax.Precision.HIGHEST, preferred_element_type=jnp.float32) / float(flat.shape[1])
    lower = jnp.linalg.cholesky(gram)
    inverse = lax.linalg.triangular_solve(lower, jnp.eye(vectors, dtype=jnp.float32), left_side=True, lower=True)
    q_block = jnp.dot(inverse.astype(jnp.float32), flat.astype(jnp.float32), precision=lax.Precision.HIGHEST, preferred_element_type=jnp.float32).reshape(updated.shape)
    return (q_block, lower.T)
```

```python
import functools
import math

import jax
import jax.numpy as jnp
from jax import lax
from jax.experimental import pallas as pl
from jax.experimental.pallas import tpu as pltpu
from jax.sharding import PartitionSpec as P

ADVECT = 0.1
DIFFUSE = 0.08
DRIVE_SCALE = 0.25
WAVENUMBER = 4.0
MESH = pl.DeviceIdType.MESH


def positions(nx, ny):
    gx, gy = lax.axis_index("gx"), lax.axis_index("gy")
    return (gx, gy, lax.rem(gx, 2) * ny + gy, gx // 2)


def plane_peer(nx, ny, step):
    gx, gy, mine, line = positions(nx, ny)
    place = lax.rem(mine + step, 2 * ny)
    return (line * 2 + place // ny, lax.rem(place, ny))


def line_peer(nx, ny, step):
    gx, gy, mine, line = positions(nx, ny)
    return (lax.rem(line + step, nx // 2) * 2 + lax.rem(gx, 2), gy)


def total_gram(nx, ny, plane, line, send_a, recv_a, send_b, recv_b):
    gx, gy, mine, place = positions(nx, ny)
    members, planes = 2 * ny, nx // 2

    def hop_a(step):
        return pltpu.make_async_remote_copy(
            plane.at[mine], plane.at[mine], send_a.at[step], recv_a.at[step],
            device_id=plane_peer(nx, ny, step), device_id_type=MESH)

    def hop_b(step):
        return pltpu.make_async_remote_copy(
            line.at[place], line.at[place], send_b.at[step], recv_b.at[step],
            device_id=line_peer(nx, ny, step), device_id_type=MESH)

    for step in range(1, members):
        hop_a(step).start()
    for step in range(1, members):
        hop_a(step).wait_recv()
    total = plane[0]
    for i in range(1, members):
        total = total + plane[i]
    line[place] = total
    for step in range(1, planes):
        hop_b(step).start()
    for step in range(1, planes):
        hop_b(step).wait_recv()
    total = line[0]
    for i in range(1, planes):
        total = total + line[i]
    for step in range(1, members):
        hop_a(step).wait_send()
    for step in range(1, planes):
        hop_b(step).wait_send()
    return total


def eliminate(gram):
    size = gram.shape[0]
    rows = lax.broadcasted_iota(jnp.int32, (size, size), 0)
    cols = lax.broadcasted_iota(jnp.int32, (size, size), 1)
    left, right = gram, (rows == cols).astype(jnp.float32)
    row = lax.broadcasted_iota(jnp.int32, (size, 1), 0)
    m = jnp.concatenate([left, right], axis=1)
    pivots = jnp.zeros((size, 1), jnp.float32)
    for k in range(size):
        pivot_row = m[k : k + 1, :]
        pivot = pivot_row[:, k : k + 1]
        column = m[:, k : k + 1]
        pivots = jnp.where(row == k, pivot, pivots)
        factor = jnp.where(row > k, column / pivot, 0.0)
        m = m - factor * pivot_row
    m = m * lax.rsqrt(pivots)
    upper = jnp.where(cols >= rows, m[:, :size], 0.0)
    return upper, m[:, size:]


def meet(nx, ny):
    barrier = pltpu.get_barrier_semaphore()
    for step in range(1, 2 * ny):
        pl.semaphore_signal(barrier, inc=1, device_id=plane_peer(nx, ny, step), device_id_type=MESH)
    for step in range(1, nx // 2):
        pl.semaphore_signal(barrier, inc=1, device_id=line_peer(nx, ny, step), device_id_type=MESH)
    pl.semaphore_wait(barrier, 2 * ny + nx // 2 - 2)


def gram_kernel(nx, ny, entries, part, upper, inverse, plane, line, send_a, recv_a, send_b, recv_b):
    meet(nx, ny)
    gx, gy, mine, place = positions(nx, ny)
    plane[mine] = part[...]
    gram = total_gram(nx, ny, plane, line, send_a, recv_a, send_b, recv_b) / entries
    upper[...], inverse[...] = eliminate(gram)


def factor_of(partial_gram, nx, ny, entries):
    size = partial_gram.shape[0]
    square = jax.ShapeDtypeStruct((size, size), jnp.float32)
    vmem = pl.BlockSpec(memory_space=pltpu.VMEM)
    return pl.pallas_call(
        functools.partial(gram_kernel, nx, ny, entries),
        out_shape=(square, square),
        in_specs=[vmem],
        out_specs=(vmem, vmem),
        scratch_shapes=[
            pltpu.VMEM((2 * ny, size, size), jnp.float32),
            pltpu.VMEM((nx // 2, size, size), jnp.float32),
            pltpu.SemaphoreType.DMA((2 * ny,)),
            pltpu.SemaphoreType.DMA((2 * ny,)),
            pltpu.SemaphoreType.DMA((nx // 2,)),
            pltpu.SemaphoreType.DMA((nx // 2,)),
        ],
        compiler_params=pltpu.CompilerParams(collective_id=0, has_side_effects=True),
    )(partial_gram)


def with_halo(value, sides, width):
    for axis, dim in sides:
        devices, length = (lax.axis_size(axis), value.shape[dim])
        up = [(i, (i + 1) % devices) for i in range(devices)]
        down = [(j, i) for i, j in up]
        last = lax.slice_in_dim(value, length - width, length, axis=dim)
        first = lax.slice_in_dim(value, 0, width, axis=dim)
        before = lax.ppermute(last, axis, up)
        after = lax.ppermute(first, axis, down)
        value = jnp.concatenate([before, value, after], axis=dim)
    return value


def advance(padded, column_index, ny_total):
    centre = padded[:, 1:-1, 1:-1, :]
    eastern = padded[:, 2:, 1:-1, :]
    western = padded[:, :-2, 1:-1, :]
    northern = padded[:, 1:-1, 2:, :]
    southern = padded[:, 1:-1, :-2, :]
    upward = jnp.roll(centre, -1, axis=3)
    downward = jnp.roll(centre, 1, axis=3)
    laplacian = eastern + western + northern + southern + upward + downward - 6.0 * centre
    advection = (
        centre[0:1] * (eastern - western)
        + centre[1:2] * (northern - southern)
        + centre[2:3] * (upward - downward)
    )
    phases = 2.0 * math.pi * WAVENUMBER * column_index.astype(jnp.float32) / float(ny_total)
    forcing = DRIVE_SCALE * jnp.sin(phases)
    nothing = jnp.zeros_like(forcing)
    driven = jnp.stack([forcing, nothing, nothing])[:, None, :, None]
    return centre + DIFFUSE * laplacian - ADVECT * advection + driven


def adjoint(base_ext, block_ext):
    inner = block_ext[:, :, 1:-1, 1:-1, :]
    base_inner = base_ext[:, 1:-1, 1:-1, :]
    base_east = base_ext[:, 2:, 1:-1, :]
    base_west = base_ext[:, :-2, 1:-1, :]
    base_north = base_ext[:, 1:-1, 2:, :]
    base_south = base_ext[:, 1:-1, :-2, :]
    block_east = block_ext[:, :, 2:, 1:-1, :]
    block_west = block_ext[:, :, :-2, 1:-1, :]
    block_north = block_ext[:, :, 1:-1, 2:, :]
    block_south = block_ext[:, :, 1:-1, :-2, :]
    carried = base_inner[2] * inner
    flux = base_east[0] * block_east - base_west[0] * block_west
    flux = flux + base_north[1] * block_north - base_south[1] * block_south
    flux = flux + jnp.roll(carried, -1, axis=-1) - jnp.roll(carried, 1, axis=-1)
    grad_x = base_east - base_west
    grad_y = base_north - base_south
    grad_z = jnp.roll(base_inner, -1, axis=3) - jnp.roll(base_inner, 1, axis=3)
    coupling = jnp.stack(
        [
            jnp.sum(inner * grad_x, axis=1),
            jnp.sum(inner * grad_y, axis=1),
            jnp.sum(inner * grad_z, axis=1),
        ],
        axis=1,
    )
    laplacian = (
        block_east
        + block_west
        + block_north
        + block_south
        + jnp.roll(inner, -1, axis=-1)
        + jnp.roll(inner, 1, axis=-1)
        - 6.0 * inner
    )
    return inner + ADVECT * (flux - coupling) + DIFFUSE * laplacian


def on_device(base_state, adjoint_block):
    vectors = adjoint_block.shape[0]
    width_y = base_state.shape[2]
    ny_total = width_y * lax.axis_size("gy")
    offset = lax.axis_index("gy") * width_y
    padded = with_halo(base_state, (("gx", 1), ("gy", 2)), 2)
    column_index = (offset + jnp.arange(-1, width_y + 1, dtype=jnp.int32)) % ny_total
    base_ext = advance(padded, column_index, ny_total)
    block_ext = with_halo(adjoint_block, (("gx", 2), ("gy", 3)), 1)
    updated = adjoint(base_ext, block_ext)
    flat = updated.reshape(vectors, -1)
    partial_gram = jnp.dot(
        flat, flat.T, precision=lax.Precision.HIGHEST, preferred_element_type=jnp.float32
    )
    entries = flat.shape[1] * lax.axis_size("gx") * lax.axis_size("gy")
    upper, inverse = factor_of(
        partial_gram, lax.axis_size("gx"), lax.axis_size("gy"), float(entries)
    )
    q_block = jnp.dot(
        inverse, flat, precision=lax.Precision.HIGHEST, preferred_element_type=jnp.float32
    ).reshape(updated.shape)
    return (q_block, upper)


def solution(mesh):
    in_specs = (P(None, "gx", "gy", None), P(None, None, "gx", "gy", None))
    out_specs = (P(None, None, "gx", "gy", None), P())
    return jax.shard_map(
        on_device, mesh=mesh, in_specs=in_specs, out_specs=out_specs, check_vma=False
    )
```

```python
import functools
import math

import jax
import jax.numpy as jnp
from jax import lax
from jax.experimental import pallas as pl
from jax.experimental.pallas import tpu as pltpu
from jax.sharding import PartitionSpec as P

ADVECT = 0.1
DIFFUSE = 0.08
DRIVE_SCALE = 0.25
WAVENUMBER = 4.0
MESH = pl.DeviceIdType.MESH


def positions(nx, ny):
    gx, gy = lax.axis_index("gx"), lax.axis_index("gy")
    return (gx, gy, lax.rem(gx, 2) * ny + gy, gx // 2)


def plane_peer(nx, ny, step):
    gx, gy, mine, line = positions(nx, ny)
    place = lax.rem(mine + step, 2 * ny)
    return (line * 2 + place // ny, lax.rem(place, ny))


def line_peer(nx, ny, step):
    gx, gy, mine, line = positions(nx, ny)
    return (lax.rem(line + step, nx // 2) * 2 + lax.rem(gx, 2), gy)


def total_gram(nx, ny, plane, line, send_a, recv_a, send_b, recv_b):
    gx, gy, mine, place = positions(nx, ny)
    members, planes = 2 * ny, nx // 2

    def hop_a(step):
        return pltpu.make_async_remote_copy(
            plane.at[mine], plane.at[mine], send_a.at[step], recv_a.at[step],
            device_id=plane_peer(nx, ny, step), device_id_type=MESH)

    def hop_b(step):
        return pltpu.make_async_remote_copy(
            line.at[place], line.at[place], send_b.at[step], recv_b.at[step],
            device_id=line_peer(nx, ny, step), device_id_type=MESH)

    for step in range(1, members):
        hop_a(step).start()
    for step in range(1, members):
        hop_a(step).wait_recv()
    total = plane[0]
    for i in range(1, members):
        total = total + plane[i]
    line[place] = total
    for step in range(1, planes):
        hop_b(step).start()
    for step in range(1, planes):
        hop_b(step).wait_recv()
    total = line[0]
    for i in range(1, planes):
        total = total + line[i]
    for step in range(1, members):
        hop_a(step).wait_send()
    for step in range(1, planes):
        hop_b(step).wait_send()
    return total


def eliminate(gram):
    size = gram.shape[0]
    rows = lax.broadcasted_iota(jnp.int32, (size, size), 0)
    cols = lax.broadcasted_iota(jnp.int32, (size, size), 1)
    left, right = gram, (rows == cols).astype(jnp.float32)
    row = lax.broadcasted_iota(jnp.int32, (size, 1), 0)
    m = jnp.concatenate([left, right], axis=1)
    pivots = jnp.zeros((size, 1), jnp.float32)
    for k in range(size):
        pivot_row = m[k : k + 1, :]
        pivot = pivot_row[:, k : k + 1]
        column = m[:, k : k + 1]
        pivots = jnp.where(row == k, pivot, pivots)
        factor = jnp.where(row > k, column / pivot, 0.0)
        m = m - factor * pivot_row
    m = m * lax.rsqrt(pivots)
    upper = jnp.where(cols >= rows, m[:, :size], 0.0)
    return upper, m[:, size:]


WIDE = 2


def neighbour(nx, ny, dx, dy):
    return (lax.rem(lax.axis_index("gx") + dx + nx, nx), lax.rem(lax.axis_index("gy") + dy + ny, ny))


SIDES = ((-1, 0), (1, 0), (0, -1), (0, 1), (-1, -1), (-1, 1), (1, -1), (1, 1))


def meet(nx, ny):
    barrier = pltpu.get_barrier_semaphore()
    peers = [neighbour(nx, ny, dx, dy) for dx, dy in SIDES if dx]
    peers += [plane_peer(nx, ny, step) for step in range(1, 2 * ny)]
    peers += [line_peer(nx, ny, step) for step in range(1, nx // 2)]
    for peer in peers:
        pl.semaphore_signal(barrier, inc=1, device_id=peer, device_id_type=MESH)
    return barrier, len(peers)


def advance_rows(bext, forcing, x, wide_y):
    rows = wide_y + 2
    centre = [bext[c, x + 1, 1 : 1 + rows, :] for c in range(3)]
    advanced = []
    for c in range(3):
        east, west = bext[c, x + 2, 1 : 1 + rows, :], bext[c, x, 1 : 1 + rows, :]
        north, south = bext[c, x + 1, 2 : 2 + rows, :], bext[c, x + 1, 0:rows, :]
        up, down = pltpu.roll(centre[c], 127, axis=1), pltpu.roll(centre[c], 1, axis=1)
        laplacian = east + west + north + south + up + down - 6.0 * centre[c]
        advection = centre[0] * (east - west) + centre[1] * (north - south) + centre[2] * (up - down)
        value = centre[c] + DIFFUSE * laplacian - ADVECT * advection
        advanced.append(value + forcing if c == 0 else value)
    return advanced


def step_kernel(
    nx, ny, entries, base, a2, q2, upper, edges, bx, by, bc, bext, adv, coef, at, split, gram_acc,
    plane, line, base_send, base_recv, halo_send, halo_recv, send_a, recv_a, send_b, recv_b,
):
    wide_x, wide_y = base.shape[1], base.shape[2]
    vectors = at.shape[3]
    stride = 3 * wide_x * wide_y
    gx, gy, mine, place = positions(nx, ny)
    barrier, met = meet(nx, ny)

    for side, start in ((0, 0), (1, wide_y - WIDE)):
        for c in range(3):
            edges[side, :, c] = base[c, :, start : start + WIDE, :]

    def move(c):
        def plane_of(x, carry):
            for y in range(wide_y):
                at[c, x + 1, y + 1] = a2[pl.ds((c * wide_x + x) * wide_y + y, vectors, stride=stride), :]
            return carry
        lax.fori_loop(0, wide_x, plane_of, 0)

    def base_copy(i):
        dx, dy = SIDES[i]
        near_x = pl.ds(0, WIDE) if dx < 0 else pl.ds(wide_x - WIDE, WIDE)
        side = 0 if dy < 0 else 1
        if dy == 0:
            src, dst = base.at[:, near_x], bx.at[(1 - dx) // 2]
        elif dx == 0:
            src, dst = edges.at[side], by.at[1 - side]
        else:
            src, dst = edges.at[side, near_x], bc.at[(1 - dx) // 2, 1 - side]
        return pltpu.make_async_remote_copy(
            src, dst, base_send.at[i], base_recv.at[i],
            device_id=neighbour(nx, ny, dx, dy), device_id_type=MESH)

    def halo_copy(c, i):
        dx, dy = SIDES[i]
        inner_x, inner_y = pl.ds(1, wide_x), pl.ds(1, wide_y)
        if dx < 0:
            src, dst = at.at[c, 1, inner_y], at.at[c, wide_x + 1, inner_y]
        elif dx > 0:
            src, dst = at.at[c, wide_x, inner_y], at.at[c, 0, inner_y]
        elif dy < 0:
            src, dst = at.at[c, inner_x, 1], at.at[c, inner_x, wide_y + 1]
        else:
            src, dst = at.at[c, inner_x, wide_y], at.at[c, inner_x, 0]
        return pltpu.make_async_remote_copy(
            src, dst, halo_send.at[c, i], halo_recv.at[c, i],
            device_id=neighbour(nx, ny, dx, dy), device_id_type=MESH)

    move(0)
    pl.semaphore_wait(barrier, met)
    for i in range(8):
        base_copy(i).start()
    for c in range(3):
        for i in range(4):
            halo_copy(c, i).start()
        if c < 2:
            move(c + 1)

    for c in range(3):
        bext[c, WIDE : WIDE + wide_x, WIDE : WIDE + wide_y, :] = base[c]
    for i in range(8):
        base_copy(i).wait_recv()
    low, high = WIDE + wide_x, WIDE + wide_y
    for c in range(3):
        for sx, start_x in ((0, 0), (1, low)):
            bext[c, start_x : start_x + WIDE, WIDE:high, :] = bx[sx, c]
            for sy, start_y in ((0, 0), (1, high)):
                bext[c, start_x : start_x + WIDE, start_y : start_y + WIDE, :] = bc[sx, sy, :, c]
        for sy, start_y in ((0, 0), (1, high)):
            bext[c, WIDE:low, start_y : start_y + WIDE, :] = by[sy, :, c]

    ny_total = wide_y * ny
    column = lax.broadcasted_iota(jnp.int32, (wide_y + 2, 128), 0) + (gy * wide_y + ny_total - 1)
    phases = 2.0 * math.pi * WAVENUMBER * lax.rem(column, ny_total).astype(jnp.float32) / float(ny_total)
    forcing = DRIVE_SCALE * jnp.sin(phases)
    for x in range(wide_x + 2):
        for c, value in enumerate(advance_rows(bext, forcing, x, wide_y)):
            adv[c, x, 0 : wide_y + 2, :] = value
    for x in range(wide_x):
        inner = [adv[m, x + 1, 1 : 1 + wide_y, :] for m in range(3)]
        coef[0, x] = ADVECT * adv[0, x + 2, 1 : 1 + wide_y, :] + DIFFUSE
        coef[1, x] = DIFFUSE - ADVECT * adv[0, x, 1 : 1 + wide_y, :]
        coef[2, x] = ADVECT * adv[1, x + 1, 2 : 2 + wide_y, :] + DIFFUSE
        coef[3, x] = DIFFUSE - ADVECT * adv[1, x + 1, 0:wide_y, :]
        coef[4, x] = ADVECT * inner[2] + DIFFUSE
        coef[5, x] = DIFFUSE - ADVECT * inner[2]
        for m in range(3):
            slopes = (
                adv[m, x + 2, 1 : 1 + wide_y, :] - adv[m, x, 1 : 1 + wide_y, :],
                adv[m, x + 1, 2 : 2 + wide_y, :] - adv[m, x + 1, 0:wide_y, :],
                pltpu.roll(inner[m], 127, axis=1) - pltpu.roll(inner[m], 1, axis=1),
            )
            for i in range(3):
                own = 1.0 - 6.0 * DIFFUSE if i == m else 0.0
                coef[6 + 3 * i + m, x] = own - ADVECT * slopes[i]

    gram_acc[...] = jnp.zeros_like(gram_acc)
    for c in range(3):
        for i in range(4):
            halo_copy(c, i).wait_recv()

        def plane_of(x, carry, c=c):
            columns = []
            for y in range(wide_y):
                k = [coef[n, x, y : y + 1, :] for n in range(6)]
                k += [coef[6 + 3 * c + m, x, y : y + 1, :] for m in range(3)]
                own = [at[m, x + 1, y + 1] for m in range(3)]
                value = k[0] * at[c, x + 2, y + 1] + k[1] * at[c, x, y + 1]
                value += k[2] * at[c, x + 1, y + 2] + k[3] * at[c, x + 1, y]
                value += pltpu.roll(k[4] * own[c], 127, axis=1) + pltpu.roll(k[5] * own[c], 1, axis=1)
                value += k[6] * own[0] + k[7] * own[1] + k[8] * own[2]
                columns.append(value)
            updated = jnp.concatenate(columns, axis=1)
            first = updated.astype(jnp.bfloat16)
            second = (updated - first.astype(jnp.float32)).astype(jnp.bfloat16)
            both = jnp.concatenate([first, second], axis=0)
            split[c * wide_x + x] = both
            gram_acc[...] += lax.dot_general(
                both, both, (((1,), (1,)), ((), ())), preferred_element_type=jnp.float32)
            return carry

        lax.fori_loop(0, wide_x, plane_of, 0)

    g = gram_acc[...]
    g = g[:vectors] + g[vectors:]
    plane[mine] = g[:, :vectors] + g[:, vectors:]
    gram = total_gram(nx, ny, plane, line, send_a, recv_a, send_b, recv_b) / entries
    upper[...], inverse = eliminate(gram)
    first = inverse.astype(jnp.bfloat16)
    second = (inverse - first.astype(jnp.float32)).astype(jnp.bfloat16)
    weights = jnp.concatenate([first, first, second, second], axis=1)

    def out_group(n, carry):
        both = split[n]
        q = jnp.dot(weights, jnp.concatenate([both, both], axis=0), preferred_element_type=jnp.float32)
        for y in range(wide_y):
            q2[pl.ds(n * wide_y + y, vectors, stride=stride), :] = q[:, y * 128 : (y + 1) * 128]
        return carry

    lax.fori_loop(0, 3 * wide_x, out_group, 0)
    for i in range(8):
        base_copy(i).wait_send()
    for c in range(3):
        for i in range(4):
            halo_copy(c, i).wait_send()


def on_device(base_state, adjoint_block):
    nx, ny = lax.axis_size("gx"), lax.axis_size("gy")
    vectors, _, wide_x, wide_y, lanes = adjoint_block.shape
    assert lanes == 128
    entries = float(3 * wide_x * wide_y * lanes * nx * ny)
    f32, dma = jnp.float32, pltpu.SemaphoreType.DMA
    vmem = pl.BlockSpec(memory_space=pltpu.VMEM)
    rows = vectors * 3 * wide_x * wide_y
    q, upper = pl.pallas_call(
        functools.partial(step_kernel, nx, ny, entries),
        out_shape=(jax.ShapeDtypeStruct((rows, 128), f32), jax.ShapeDtypeStruct((vectors, vectors), f32)),
        in_specs=[vmem, vmem],
        out_specs=(vmem, vmem),
        scratch_shapes=[
            pltpu.VMEM((2, wide_x, 3, WIDE, 128), f32),
            pltpu.VMEM((2, 3, WIDE, wide_y, 128), f32),
            pltpu.VMEM((2, wide_x, 3, WIDE, 128), f32),
            pltpu.VMEM((2, 2, WIDE, 3, WIDE, 128), f32),
            pltpu.VMEM((3, wide_x + 4, wide_y + 8, 128), f32),
            pltpu.VMEM((3, wide_x + 2, wide_y + 8, 128), f32),
            pltpu.VMEM((15, wide_x, wide_y, 128), f32),
            pltpu.VMEM((3, wide_x + 2, wide_y + 2, vectors, 128), f32),
            pltpu.VMEM((3 * wide_x, 2 * vectors, wide_y * 128), jnp.bfloat16),
            pltpu.VMEM((2 * vectors, 2 * vectors), f32),
            pltpu.VMEM((2 * ny, vectors, vectors), f32),
            pltpu.VMEM((nx // 2, vectors, vectors), f32),
            dma((8,)), dma((8,)), dma((3, 4)), dma((3, 4)),
            dma((2 * ny,)), dma((2 * ny,)), dma((nx // 2,)), dma((nx // 2,)),
        ],
        compiler_params=pltpu.CompilerParams(collective_id=0, has_side_effects=True),
    )(base_state, adjoint_block.reshape(rows, 128))
    return (q.reshape(adjoint_block.shape), upper)


def solution(mesh):
    in_specs = (P(None, "gx", "gy", None), P(None, None, "gx", "gy", None))
    out_specs = (P(None, None, "gx", "gy", None), P())
    return jax.shard_map(
        on_device, mesh=mesh, in_specs=in_specs, out_specs=out_specs, check_vma=False
    )
```

```python
import functools
import math

import jax
import jax.numpy as jnp
from jax import lax
from jax.experimental import pallas as pl
from jax.experimental.pallas import tpu as pltpu
from jax.sharding import PartitionSpec as P

ADVECT = 0.1
DIFFUSE = 0.08
DRIVE_SCALE = 0.25
WAVENUMBER = 4.0
MESH = pl.DeviceIdType.MESH


def positions(nx, ny):
    gx, gy = lax.axis_index("gx"), lax.axis_index("gy")
    return (gx, gy, lax.rem(gx, 2) * ny + gy, gx // 2)


def plane_peer(nx, ny, step):
    gx, gy, mine, line = positions(nx, ny)
    place = lax.rem(mine + step, 2 * ny)
    return (line * 2 + place // ny, lax.rem(place, ny))


def line_peer(nx, ny, step):
    gx, gy, mine, line = positions(nx, ny)
    return (lax.rem(line + step, nx // 2) * 2 + lax.rem(gx, 2), gy)


def total_gram(nx, ny, plane, line, send_a, recv_a, send_b, recv_b):
    gx, gy, mine, place = positions(nx, ny)
    members, planes = 2 * ny, nx // 2

    def hop_a(step):
        return pltpu.make_async_remote_copy(
            plane.at[mine], plane.at[mine], send_a.at[step], recv_a.at[step],
            device_id=plane_peer(nx, ny, step), device_id_type=MESH)

    def hop_b(step):
        return pltpu.make_async_remote_copy(
            line.at[place], line.at[place], send_b.at[step], recv_b.at[step],
            device_id=line_peer(nx, ny, step), device_id_type=MESH)

    for step in range(1, members):
        hop_a(step).start()
    for step in range(1, members):
        hop_a(step).wait_recv()
    total = plane[0]
    for i in range(1, members):
        total = total + plane[i]
    line[place] = total
    for step in range(1, planes):
        hop_b(step).start()
    for step in range(1, planes):
        hop_b(step).wait_recv()
    total = line[0]
    for i in range(1, planes):
        total = total + line[i]
    for step in range(1, members):
        hop_a(step).wait_send()
    for step in range(1, planes):
        hop_b(step).wait_send()
    return total


def eliminate(gram):
    size = gram.shape[0]
    rows = lax.broadcasted_iota(jnp.int32, (size, size), 0)
    cols = lax.broadcasted_iota(jnp.int32, (size, size), 1)
    left, right = gram, (rows == cols).astype(jnp.float32)
    row = lax.broadcasted_iota(jnp.int32, (size, 1), 0)
    m = jnp.concatenate([left, right], axis=1)
    pivots = jnp.zeros((size, 1), jnp.float32)
    for k in range(size):
        pivot_row = m[k : k + 1, :]
        pivot = pivot_row[:, k : k + 1]
        column = m[:, k : k + 1]
        pivots = jnp.where(row == k, pivot, pivots)
        factor = jnp.where(row > k, column / pivot, 0.0)
        m = m - factor * pivot_row
    m = m * lax.rsqrt(pivots)
    upper = jnp.where(cols >= rows, m[:, :size], 0.0)
    return upper, m[:, size:]


WIDE = 2


def neighbour(nx, ny, dx, dy):
    return (lax.rem(lax.axis_index("gx") + dx + nx, nx), lax.rem(lax.axis_index("gy") + dy + ny, ny))


SIDES = ((-1, 0), (1, 0), (0, -1), (0, 1), (-1, -1), (-1, 1), (1, -1), (1, 1))


def meet(nx, ny):
    barrier = pltpu.get_barrier_semaphore()
    peers = [neighbour(nx, ny, dx, dy) for dx, dy in SIDES if dx]
    peers += [plane_peer(nx, ny, step) for step in range(1, 2 * ny)]
    peers += [line_peer(nx, ny, step) for step in range(1, nx // 2)]
    for peer in peers:
        pl.semaphore_signal(barrier, inc=1, device_id=peer, device_id_type=MESH)
    return barrier, len(peers)


def advance_rows(bext, forcing, x, wide_y):
    rows = wide_y + 2
    centre = [bext[c, x + 1, 1 : 1 + rows, :] for c in range(3)]
    advanced = []
    for c in range(3):
        east, west = bext[c, x + 2, 1 : 1 + rows, :], bext[c, x, 1 : 1 + rows, :]
        north, south = bext[c, x + 1, 2 : 2 + rows, :], bext[c, x + 1, 0:rows, :]
        up, down = pltpu.roll(centre[c], 127, axis=1), pltpu.roll(centre[c], 1, axis=1)
        laplacian = east + west + north + south + up + down - 6.0 * centre[c]
        advection = centre[0] * (east - west) + centre[1] * (north - south) + centre[2] * (up - down)
        value = centre[c] + DIFFUSE * laplacian - ADVECT * advection
        advanced.append(value + forcing if c == 0 else value)
    return advanced


def step_kernel(
    nx, ny, entries, base_in, a_in, pieces, gram, base, a2, in_sem, edges, bx, by, bc, bext, adv, coef, at, split, gram_acc,
    plane, line, base_send, base_recv, halo_send, halo_recv, send_a, recv_a, send_b, recv_b, out_sem,
):
    wide_x, wide_y = base.shape[1], base.shape[2]
    vectors = at.shape[3]
    stride = 3 * wide_x * wide_y
    gx, gy, mine, place = positions(nx, ny)
    barrier, met = meet(nx, ny)
    base_load = pltpu.make_async_copy(base_in, base, in_sem.at[0])
    load = pltpu.make_async_copy(a_in, a2, in_sem.at[1])
    base_load.start()
    load.start()
    base_load.wait()

    for side, start in ((0, 0), (1, wide_y - WIDE)):
        for c in range(3):
            edges[side, :, c] = base[c, :, start : start + WIDE, :]

    def move(c):
        def plane_of(x, carry):
            for y in range(wide_y):
                at[c, x + 1, y + 1] = a2[pl.ds((c * wide_x + x) * wide_y + y, vectors, stride=stride), :]
            return carry
        lax.fori_loop(0, wide_x, plane_of, 0)

    def base_copy(i):
        dx, dy = SIDES[i]
        near_x = pl.ds(0, WIDE) if dx < 0 else pl.ds(wide_x - WIDE, WIDE)
        side = 0 if dy < 0 else 1
        if dy == 0:
            src, dst = base.at[:, near_x], bx.at[(1 - dx) // 2]
        elif dx == 0:
            src, dst = edges.at[side], by.at[1 - side]
        else:
            src, dst = edges.at[side, near_x], bc.at[(1 - dx) // 2, 1 - side]
        return pltpu.make_async_remote_copy(
            src, dst, base_send.at[i], base_recv.at[i],
            device_id=neighbour(nx, ny, dx, dy), device_id_type=MESH)

    def halo_copy(c, i):
        dx, dy = SIDES[i]
        inner_x, inner_y = pl.ds(1, wide_x), pl.ds(1, wide_y)
        if dx < 0:
            src, dst = at.at[c, 1, inner_y], at.at[c, wide_x + 1, inner_y]
        elif dx > 0:
            src, dst = at.at[c, wide_x, inner_y], at.at[c, 0, inner_y]
        elif dy < 0:
            src, dst = at.at[c, inner_x, 1], at.at[c, inner_x, wide_y + 1]
        else:
            src, dst = at.at[c, inner_x, wide_y], at.at[c, inner_x, 0]
        return pltpu.make_async_remote_copy(
            src, dst, halo_send.at[c, i], halo_recv.at[c, i],
            device_id=neighbour(nx, ny, dx, dy), device_id_type=MESH)

    pl.semaphore_wait(barrier, met)
    for i in range(8):
        base_copy(i).start()
    load.wait()
    move(0)
    for c in range(3):
        for i in range(4):
            halo_copy(c, i).start()
        if c < 2:
            move(c + 1)

    for c in range(3):
        bext[c, WIDE : WIDE + wide_x, WIDE : WIDE + wide_y, :] = base[c]
    for i in range(8):
        base_copy(i).wait_recv()
    low, high = WIDE + wide_x, WIDE + wide_y
    for c in range(3):
        for sx, start_x in ((0, 0), (1, low)):
            bext[c, start_x : start_x + WIDE, WIDE:high, :] = bx[sx, c]
            for sy, start_y in ((0, 0), (1, high)):
                bext[c, start_x : start_x + WIDE, start_y : start_y + WIDE, :] = bc[sx, sy, :, c]
        for sy, start_y in ((0, 0), (1, high)):
            bext[c, WIDE:low, start_y : start_y + WIDE, :] = by[sy, :, c]

    ny_total = wide_y * ny
    column = lax.broadcasted_iota(jnp.int32, (wide_y + 2, 128), 0) + (gy * wide_y + ny_total - 1)
    phases = 2.0 * math.pi * WAVENUMBER * lax.rem(column, ny_total).astype(jnp.float32) / float(ny_total)
    forcing = DRIVE_SCALE * jnp.sin(phases)
    for x in range(wide_x + 2):
        for c, value in enumerate(advance_rows(bext, forcing, x, wide_y)):
            adv[c, x, 0 : wide_y + 2, :] = value
    for x in range(wide_x):
        inner = [adv[m, x + 1, 1 : 1 + wide_y, :] for m in range(3)]
        coef[0, x] = ADVECT * adv[0, x + 2, 1 : 1 + wide_y, :] + DIFFUSE
        coef[1, x] = DIFFUSE - ADVECT * adv[0, x, 1 : 1 + wide_y, :]
        coef[2, x] = ADVECT * adv[1, x + 1, 2 : 2 + wide_y, :] + DIFFUSE
        coef[3, x] = DIFFUSE - ADVECT * adv[1, x + 1, 0:wide_y, :]
        coef[4, x] = ADVECT * inner[2] + DIFFUSE
        coef[5, x] = DIFFUSE - ADVECT * inner[2]
        for m in range(3):
            slopes = (
                adv[m, x + 2, 1 : 1 + wide_y, :] - adv[m, x, 1 : 1 + wide_y, :],
                adv[m, x + 1, 2 : 2 + wide_y, :] - adv[m, x + 1, 0:wide_y, :],
                pltpu.roll(inner[m], 127, axis=1) - pltpu.roll(inner[m], 1, axis=1),
            )
            for i in range(3):
                own = 1.0 - 6.0 * DIFFUSE if i == m else 0.0
                coef[6 + 3 * i + m, x] = own - ADVECT * slopes[i]

    def out_copy(c):
        part = pl.ds(c * wide_x, wide_x)
        return pltpu.make_async_copy(split.at[part], pieces.at[part], out_sem.at[c])

    gram_acc[...] = jnp.zeros_like(gram_acc)
    for c in range(3):
        for i in range(4):
            halo_copy(c, i).wait_recv()

        def plane_of(x, carry, c=c):
            columns = []
            for y in range(wide_y):
                k = [coef[n, x, y : y + 1, :] for n in range(6)]
                k += [coef[6 + 3 * c + m, x, y : y + 1, :] for m in range(3)]
                own = [at[m, x + 1, y + 1] for m in range(3)]
                value = k[0] * at[c, x + 2, y + 1] + k[1] * at[c, x, y + 1]
                value += k[2] * at[c, x + 1, y + 2] + k[3] * at[c, x + 1, y]
                value += pltpu.roll(k[4] * own[c], 127, axis=1) + pltpu.roll(k[5] * own[c], 1, axis=1)
                value += k[6] * own[0] + k[7] * own[1] + k[8] * own[2]
                columns.append(value)
            updated = jnp.concatenate(columns, axis=1)
            first = updated.astype(jnp.bfloat16)
            second = (updated - first.astype(jnp.float32)).astype(jnp.bfloat16)
            both = jnp.concatenate([first, second], axis=0)
            split[c * wide_x + x] = both
            gram_acc[...] += lax.dot_general(
                both, both, (((1,), (1,)), ((), ())), preferred_element_type=jnp.float32)
            return carry

        lax.fori_loop(0, wide_x, plane_of, 0)
        if c:
            out_copy(c - 1).start()

    g = gram_acc[...]
    g = g[:vectors] + g[vectors:]
    plane[mine] = g[:, :vectors] + g[:, vectors:]
    out_copy(2).start()
    gram[...] = total_gram(nx, ny, plane, line, send_a, recv_a, send_b, recv_b) / entries
    for c in range(3):
        out_copy(c).wait()
    for i in range(8):
        base_copy(i).wait_send()
    for c in range(3):
        for i in range(4):
            halo_copy(c, i).wait_send()


def factor_kernel(gram, pieces, q, upper, split, result, in_sem, out_sem):
    groups, vectors, wide_y = q.shape[1], q.shape[0], q.shape[2]

    def load(n):
        return pltpu.make_async_copy(pieces.at[n], split.at[n], in_sem.at[n])

    def store(n):
        return pltpu.make_async_copy(result.at[:, n], q.at[:, n], out_sem.at[n])

    def over(body):
        def run(n, carry):
            body(n)
            return carry
        lax.fori_loop(0, groups, run, 0)

    over(lambda n: load(n).start())
    upper[...], inverse = eliminate(gram[...])
    first = inverse.astype(jnp.bfloat16)
    second = (inverse - first.astype(jnp.float32)).astype(jnp.bfloat16)
    weights = jnp.concatenate([first, first, second, second], axis=1)
    flat = result.reshape(vectors * groups * wide_y, 128)

    def group(n):
        load(n).wait()
        both = split[n]
        value = jnp.dot(weights, jnp.concatenate([both, both], axis=0), preferred_element_type=jnp.float32)
        for y in range(wide_y):
            flat[pl.ds(n * wide_y + y, vectors, stride=groups * wide_y), :] = value[:, y * 128 : (y + 1) * 128]
        store(n).start()

    over(group)
    over(lambda n: store(n).wait())


def on_device(base_state, adjoint_block):
    nx, ny = lax.axis_size("gx"), lax.axis_size("gy")
    vectors, _, wide_x, wide_y, lanes = adjoint_block.shape
    assert lanes == 128
    entries = float(3 * wide_x * wide_y * lanes * nx * ny)
    f32, dma = jnp.float32, pltpu.SemaphoreType.DMA
    vmem = pl.BlockSpec(memory_space=pltpu.VMEM)
    rows = vectors * 3 * wide_x * wide_y
    split_shape = (3 * wide_x, 2 * vectors, wide_y * 128)
    any_space = pl.BlockSpec(memory_space=pl.ANY)
    pieces, gram = pl.pallas_call(
        functools.partial(step_kernel, nx, ny, entries),
        out_shape=(jax.ShapeDtypeStruct(split_shape, jnp.bfloat16), jax.ShapeDtypeStruct((vectors, vectors), f32)),
        in_specs=[any_space, any_space],
        out_specs=(any_space, vmem),
        scratch_shapes=[
            pltpu.VMEM(base_state.shape, f32),
            pltpu.VMEM((rows, 128), f32),
            dma((2,)),
            pltpu.VMEM((2, wide_x, 3, WIDE, 128), f32),
            pltpu.VMEM((2, 3, WIDE, wide_y, 128), f32),
            pltpu.VMEM((2, wide_x, 3, WIDE, 128), f32),
            pltpu.VMEM((2, 2, WIDE, 3, WIDE, 128), f32),
            pltpu.VMEM((3, wide_x + 4, wide_y + 8, 128), f32),
            pltpu.VMEM((3, wide_x + 2, wide_y + 8, 128), f32),
            pltpu.VMEM((15, wide_x, wide_y, 128), f32),
            pltpu.VMEM((3, wide_x + 2, wide_y + 2, vectors, 128), f32),
            pltpu.VMEM(split_shape, jnp.bfloat16),
            pltpu.VMEM((2 * vectors, 2 * vectors), f32),
            pltpu.VMEM((2 * ny, vectors, vectors), f32),
            pltpu.VMEM((nx // 2, vectors, vectors), f32),
            dma((8,)), dma((8,)), dma((3, 4)), dma((3, 4)),
            dma((2 * ny,)), dma((2 * ny,)), dma((nx // 2,)), dma((nx // 2,)), dma((3,)),
        ],
        compiler_params=pltpu.CompilerParams(collective_id=0, has_side_effects=True),
    )(base_state, adjoint_block.reshape(rows, 128))
    q_shape = (vectors, 3 * wide_x, wide_y, 128)
    q, upper = pl.pallas_call(
        factor_kernel,
        out_shape=(jax.ShapeDtypeStruct(q_shape, f32), jax.ShapeDtypeStruct((vectors, vectors), f32)),
        in_specs=[vmem, any_space],
        out_specs=(any_space, vmem),
        scratch_shapes=[
            pltpu.VMEM(split_shape, jnp.bfloat16),
            pltpu.VMEM(q_shape, f32),
            dma((3 * wide_x,)), dma((3 * wide_x,)),
        ],
    )(gram, pieces)
    return (q.reshape(adjoint_block.shape), upper)


def solution(mesh):
    in_specs = (P(None, "gx", "gy", None), P(None, None, "gx", "gy", None))
    out_specs = (P(None, None, "gx", "gy", None), P())
    return jax.shard_map(
        on_device, mesh=mesh, in_specs=in_specs, out_specs=out_specs, check_vma=False
    )
```
